32 devices in a mesh: row: 4 (over z), col: 8 (over y, x, core).
Axes of the slice: x: 2, y: 2, z: 4, core: 2. Of those that a mesh axis runs over, the one named last changes fastest.
Arguments:
- splat_params: float32 [10, 2097152], P(None, ('row', 'col')), as said below
- list_owner: int32 [128, 1024, 1], P(('row', 'col')), may hold values from 0 to 31; in each aligned block of 4096 rows (0 to 4095, 4096 to 8191, ..., all dimensions but the last counted through in order) at most 256 rows name the same one
- list_slot: int32 [128, 1024], P(('row', 'col')), may hold values from 0 to 65535
- list_length: int32 [128], P(('row', 'col')), may hold values from 512 to 1024, as said below
- target: float32 [4, 128, 256], P(None, ('row', 'col')), may hold values from 0 to 1
Outputs:
- rendered: float32 [4, 128, 256], P(None, ('row', 'col'))
- splat_grads: float32 [10, 2097152], P(None, ('row', 'col'))
The draws below stay inside these ranges and needn't reach their ends.
Inputs may be any that keep to these rules, and one draw needn't show every extreme that they name: `list_owner`: within the entries of one device's tiles (aligned blocks of 4096 entries), no owner is named more than 256 times, a bound that some block reaches. `list_length`: some tile has exactly 1024 live entries; every tile has at least 512. `splat_params`: conic entries satisfy a > 0, c > 0 and b * b < a * c; opacity lies in (0, 0.02]; colours and depth lie in [0, 1].
All inputs are finite; a program needn't handle non-finite values.
Results may differ from the reference program's by a relative error of at most 0.0003.
Values sent between devices are 32-bit elements; how exact they have to be, the bound alone decides.
A program may use at most 128 MiB of HBM per device.

```python
import math
import jax
import jax.numpy as jnp
import numpy as np
from jax import lax

SIDE = 16
PIX = 256
K = 1024
TILE_DEV = 4
G_DEV = 65536
TILES = 128
GROUP_TILES = 32
SPLATS = 2097152
CAP = 256
DEVICES = 32


def log_uniform(key, shape, low, high):
    return jnp.exp(jax.random.uniform(key, shape, jnp.float32, jnp.log(low), jnp.log(high)))


def draw_splat_params(key, part):
    keys = jax.random.split(key, 8)
    shape = (SPLATS,)
    mean_x = jax.random.uniform(keys[0], shape, jnp.float32, -2.0, 18.0)
    mean_y = jax.random.uniform(keys[1], shape, jnp.float32, -2.0, 18.0)
    conic_a = log_uniform(keys[2], shape, 0.05, 0.5)
    conic_c = log_uniform(keys[3], shape, 0.05, 0.5)
    conic_b = jax.random.uniform(keys[4], shape, jnp.float32, -0.6, 0.6) * jnp.sqrt(conic_a * conic_c)
    opacity = log_uniform(keys[5], shape, 0.002, 0.02)
    colours = jax.random.uniform(keys[6], (3, SPLATS), jnp.float32)
    depth = log_uniform(keys[7], shape, 0.05, 1.0)
    geometry = jnp.stack([mean_x, mean_y, conic_a, conic_b, conic_c, opacity])
    return jnp.concatenate([geometry, colours, depth[None, :]], axis=0)


def draw_list_length(key, part):
    tile_index = jnp.arange(TILES, dtype=jnp.int32)
    groups = TILES // GROUP_TILES
    group = tile_index // GROUP_TILES
    heavy = jax.random.randint(jax.random.fold_in(key, 11), (), 0, groups)
    is_heavy = group == heavy
    longest = jnp.where(is_heavy, K, 3 * K // 4).astype(jnp.int32)
    shortest = jnp.where(is_heavy, 7 * K // 8, K // 2).astype(jnp.int32)
    lengths = jax.random.randint(jax.random.fold_in(key, 12), (TILES,), shortest, longest + 1)
    return jnp.where(tile_index == heavy * GROUP_TILES, K, lengths).astype(jnp.int32)


def place_ends(array, rng, least, high):
    dims = array.shape
    spot = [jax.random.randint(jax.random.fold_in(rng, axis), (), 0, dims[axis]) for axis in range(len(dims))]
    array = array.at[tuple(spot)].set(least)
    longest = dims.index(max(dims))
    spot[longest] = (spot[longest] + 1) % dims[longest]
    return array.at[tuple(spot)].set(high)


def block_scale(own_key, dims, cuts, low, top_value):
    factor_of = 1.0
    for axis_at, blocks in cuts:
        draws = jax.random.uniform(jax.random.fold_in(jax.random.fold_in(own_key, 6), axis_at), (blocks,), jnp.float32, low / len(cuts), top_value / len(cuts))
        factor_of = factor_of * jnp.repeat(jnp.exp(draws), dims[axis_at] // blocks).reshape((-1,) + (1,) * (len(dims) - 1 - axis_at))
    return factor_of


def shared_out(rng, own, number, rows, count, top, most, lean):
    order = jax.random.permutation(rng, count)
    crowded, common = shares(count, rows * top, most, lean, True), shares(count, rows * top, most, lean, False)
    places = jnp.arange(count)

    def named(sizes, turn):
        used = int((sizes > 0).sum())
        fixed = max(1, used // 4)
        moved = fixed + (places - fixed + turn * (used - fixed)) % max(1, count - fixed)
        return jnp.zeros((count,), jnp.int32).at[order[jnp.where(places < fixed, places, moved)]].set(jnp.asarray(sizes, jnp.int32))

    sizes = jnp.where(number % 4 == 0, named(crowded, number // 4), named(common, number - number // 4 - 1))
    mixed = jax.random.permutation(jax.random.fold_in(own, 3), count)
    source_of, receiver = mixed[0:count // 2 * 2:2], mixed[1:count // 2 * 2:2]
    slack = jnp.minimum(sizes[source_of] - 1, most - sizes[receiver]) // 2
    slack = jnp.where((source_of == order[0]) | (receiver == order[0]) | (sizes[receiver] == 0), 0, jnp.maximum(slack, 0))
    moved = jax.random.randint(jax.random.fold_in(own, 4), (count // 2,), 0, 1 << 20) % (slack + 1)
    sizes = sizes.at[source_of].add(-moved).at[receiver].add(moved)
    labels = jnp.searchsorted(jnp.cumsum(sizes), jnp.arange(rows * top), side="right").astype(jnp.int32)
    table = labels.reshape(top, rows).T
    table = table[jax.random.permutation(jax.random.fold_in(own, 1), rows)]
    turn = jax.random.randint(jax.random.fold_in(own, 2), (rows, 1), 0, top)
    return jnp.take_along_axis(table, (jnp.arange(top)[None, :] + turn) % top, axis=1)


def shares(amount, total, most, skew, full):
    loads = [(1 << 20) // math.isqrt(standing ** skew) + 1 for standing in range(1, amount + 1)]
    largest = most if full else min(most, max(-(-total // amount), total * loads[0] // sum(loads)))
    least = 1 if total - largest >= amount - 1 else 0
    counts, rest = [largest] + [least] * (amount - 1), total - largest - least * (amount - 1)
    while rest > 0:
        free = [i for i in range(1, amount) if counts[i] < largest] or [i for i in range(1, amount) if counts[i] < most]
        whole, left = sum([loads[i] for i in free]), rest
        for i in free:
            extra = min(most - counts[i], max(1, left * loads[i] // whole), rest)
            counts[i] = counts[i] + extra
            rest = rest - extra
    return np.array(counts)


def setup_inputs(seed: int = 0) -> dict:
    seeds = jax.random.split(jax.random.key(seed), 6)
    splat_params = draw_splat_params(jax.random.fold_in(seeds[5], 71), 0)
    list_owner_keys = jax.random.split(jax.random.fold_in(seeds[1], 1), TILES * K // (TILE_DEV * K))
    list_owner_turns = jax.random.permutation(jax.random.fold_in(seeds[1], 3), TILES * K // (TILE_DEV * K))
    list_owner = jax.vmap(lambda own, number: shared_out(jax.random.fold_in(seeds[1], 2), own, number, TILE_DEV * K, DEVICES, 1, CAP, 2))(list_owner_keys, list_owner_turns).reshape((TILES, K, 1))
    list_slot = place_ends(jax.random.randint(seeds[2], (TILES, K), 0, G_DEV), jax.random.fold_in(seeds[2], 1), 0, G_DEV - 1).astype(jnp.int32)
    list_length = draw_list_length(jax.random.fold_in(seeds[5], 71), 0)
    target = jnp.clip(1.0 * jax.random.uniform(seeds[4], (4, TILES, PIX), jnp.float32) ** block_scale(seeds[4], (4, TILES, PIX), ((1, 32),), -0.2, 0.2), 0.0, 1.0)
    return dict(splat_params=splat_params, list_owner=list_owner, list_slot=list_slot, list_length=list_length, target=target)


precise = lax.Precision.HIGHEST


def render_tile(values, length, tile_target):
    pixel_index = jnp.arange(PIX)
    pixel_x = (pixel_index % SIDE).astype(jnp.float32) + 0.5
    pixel_y = (pixel_index // SIDE).astype(jnp.float32) + 0.5
    live_mask = (jnp.arange(K) < length).astype(jnp.float32)
    mean_x = values[0]
    mean_y = values[1]
    conic_a = values[2]
    conic_b = values[3]
    conic_c = values[4]
    opacity = values[5] * live_mask
    colours = values[6:10]
    offset_x = pixel_x[:, None] - mean_x[None, :]
    offset_y = pixel_y[:, None] - mean_y[None, :]
    exponent = 0.5 * (conic_a * offset_x * offset_x + conic_c * offset_y * offset_y) + conic_b * offset_x * offset_y
    falloff = jnp.exp(-exponent)
    alphas = opacity[None, :] * falloff
    log_keep = jnp.log1p(-alphas)
    log_trans = jnp.cumsum(log_keep, axis=1) - log_keep
    transmit = jnp.exp(log_trans)
    weight = alphas * transmit
    rendered = jnp.dot(colours, weight.T, precision=precise)
    grad_image = 2.0 * (rendered - tile_target)
    grad_colours = jnp.dot(grad_image, weight, precision=precise)
    shading = jnp.dot(grad_image.T, colours, precision=precise)
    spent_sum = weight * shading
    before = jnp.cumsum(spent_sum, axis=1)
    grand_total = jnp.sum(grad_image * rendered, axis=0)
    grad_alpha = transmit * shading - (grand_total[:, None] - before) / (1.0 - alphas)
    grad_power = -grad_alpha * alphas
    grad_mean_x = jnp.sum(-grad_power * (conic_a * offset_x + conic_b * offset_y), axis=0)
    grad_mean_y = jnp.sum(-grad_power * (conic_c * offset_y + conic_b * offset_x), axis=0)
    grad_a = jnp.sum(grad_power * 0.5 * offset_x * offset_x, axis=0)
    grad_b = jnp.sum(grad_power * offset_x * offset_y, axis=0)
    grad_c = jnp.sum(grad_power * 0.5 * offset_y * offset_y, axis=0)
    grad_opacity = jnp.sum(grad_alpha * falloff, axis=0) * live_mask
    geometry_grads = jnp.stack([grad_mean_x, grad_mean_y, grad_a, grad_b, grad_c, grad_opacity])
    return rendered, jnp.concatenate([geometry_grads, grad_colours], axis=0)


def reference(splat_params, list_owner, list_slot, list_length, target):
    splat_ids = (list_owner[:, :, 0] * G_DEV + list_slot).astype(jnp.int32)

    def render_one(tile_step):
        values = jnp.take(splat_params, splat_ids[tile_step], axis=1)
        return render_tile(values, list_length[tile_step], target[:, tile_step, :])

    images, entry_grads = lax.map(render_one, jnp.arange(TILES, dtype=jnp.int32))
    rendered = jnp.transpose(images, (1, 0, 2))
    flat_grads = jnp.transpose(entry_grads, (1, 0, 2)).reshape(10, TILES * K)
    splat_grads = jnp.zeros((10, SPLATS), jnp.float32).at[:, splat_ids.reshape(-1)].add(flat_grads)
    return rendered, splat_grads
```

```python
import functools

import jax
import jax.numpy as jnp
from jax import lax
from jax.experimental import pallas as pl
from jax.experimental.pallas import tpu as pltpu
from jax.sharding import PartitionSpec as P

SIDE = 16
SB = 256
LANES = 256
CH = 10
F32 = jnp.float32
BF16 = jnp.bfloat16
NT = (((1,), (1,)), ((), ()))


def iota(shape, dim):
    return lax.broadcasted_iota(jnp.int32, shape, dim)


def split(x):
    high = x.astype(BF16)
    return high, (x - high.astype(F32)).astype(BF16)


def mm(a, b):
    return jnp.dot(a, b, preferred_element_type=F32)


def mm_nt(a, b):
    return lax.dot_general(a, b, NT, preferred_element_type=F32)


def one_hot(index, size):
    return jnp.where(iota((size, index.shape[1]), 0) == index, 1.0, 0.0).astype(BF16)


def plan_kernel(own_ref, slot_ref, req_ref, rank_ref):
    devices, cap = req_ref.shape
    entries = own_ref.shape[1]
    strict = jnp.where(iota((SB, SB), 0) < iota((SB, SB), 1), 1.0, 0.0).astype(BF16)
    carry = jnp.zeros((devices, 1), F32)
    high = jnp.zeros((devices, cap), F32)
    low = jnp.zeros((devices, cap), F32)
    for j in range(entries // SB):
        part = slice(j * SB, (j + 1) * SB)
        mine = iota((devices, SB), 0) == own_ref[:, part]
        ones = jnp.where(mine, 1.0, 0.0)
        count = mm(ones.astype(BF16), strict) + carry
        rank = jnp.sum(ones * count, axis=0, keepdims=True).astype(jnp.int32)
        carry = carry + jnp.sum(ones, axis=1, keepdims=True)
        rank_ref[:, part] = rank
        slots = slot_ref[:, part]
        places = one_hot(rank, cap)
        slot_high = (slots >> 8).astype(F32)
        slot_low = (slots & 255).astype(F32)
        high = high + mm_nt(jnp.where(mine, slot_high, 0.0).astype(BF16), places)
        low = low + mm_nt(jnp.where(mine, slot_low, 0.0).astype(BF16), places)
    req_ref[...] = (high * 256.0 + low).astype(jnp.int32)


def gather_kernel(ask_ref, table_ref, out_ref, high_ref, low_ref):
    width = table_ref.shape[1]
    rows = table_ref.shape[0] // CH

    @pl.when(pl.program_id(0) == 0)
    def _():
        for ch in range(CH):
            part = slice(ch * rows, (ch + 1) * rows)
            high, low = split(table_ref[part, :])
            high_ref[part, :] = high
            low_ref[part, :] = low

    index = ask_ref[0]
    column = one_hot(index & (width - 1), width)
    row = iota((rows, index.shape[1]), 0) == (index >> 8)
    for ch in range(CH):
        part = slice(ch * rows, (ch + 1) * rows)
        found = mm(high_ref[part, :], column) + mm(low_ref[part, :], column)
        out_ref[0, ch : ch + 1, :] = jnp.sum(jnp.where(row, found, 0.0), axis=0, keepdims=True)


def render_kernel(
    length_ref, own_ref, rank_ref, reply_ref, target_ref, image_ref, out_ref,
    vals, grads, falloff_ref, trans_ref, high_ref, low_ref, shade_ref, before_ref,
):
    tile = pl.program_id(0)
    devices = reply_ref.shape[0] // CH
    cap = reply_ref.shape[1]
    slots = own_ref.shape[2]
    pixels = target_ref.shape[2]
    blocks = slots // SB
    length = length_ref[tile]
    mine = iota((devices, slots), 0) == own_ref[0]
    places = one_hot(rank_ref[0], cap)
    reply_high, reply_low = split(reply_ref[...])
    vals[...] = jnp.zeros_like(vals)
    live = jnp.where(iota((1, slots), 1) < length, 1.0, 0.0)
    for ch in range(CH):
        part = slice(ch * devices, (ch + 1) * devices)
        found = mm(reply_high[part], places) + mm(reply_low[part], places)
        value = jnp.sum(jnp.where(mine, found, 0.0), axis=0, keepdims=True)
        if ch == 5:
            value = value * live
        row = ch if ch < 6 else ch + 2
        vals[row : row + 1, :] = value

    strict = jnp.where(iota((SB, SB), 0) < iota((SB, SB), 1), 1.0, 0.0).astype(BF16)
    inclusive = jnp.where(iota((SB, SB), 0) <= iota((SB, SB), 1), 1.0, 0.0).astype(BF16)
    centres = iota((SIDE, SB), 0).astype(F32) + 0.5
    side_rows = pixels // SIDE

    carry = jnp.zeros((pixels, 1), F32)
    image = jnp.zeros((8, pixels), F32)
    for blk in range(blocks):
        at = slice(blk * SB, (blk + 1) * SB)
        dx = centres - vals[0:1, at]
        dy = centres - vals[1:2, at]
        ex = 0.5 * vals[2:3, at] * dx * dx
        ey = 0.5 * vals[4:5, at] * dy * dy
        bdy = vals[3:4, at] * dy
        opacity = vals[5:6, at]
        for y in range(side_rows):
            rows = slice(y * SIDE, (y + 1) * SIDE)
            exponent = ex + ey[y : y + 1] + dx * bdy[y : y + 1]
            falloff = jnp.exp(-exponent)
            falloff_ref[rows, at] = falloff
            keep = jnp.log(1.0 - opacity * falloff)
            high, low = split(keep)
            high_ref[rows, :] = high
            low_ref[rows, :] = low
        total = mm(high_ref[...], strict) + mm(low_ref[...], strict) + carry
        last = high_ref[:, SB - 128 :].astype(F32) + low_ref[:, SB - 128 :].astype(F32)
        carry = total[:, SB - 1 : SB] + last[:, 127:128]
        trans = jnp.exp(total)
        trans_ref[:, at] = trans
        weight_high, weight_low = split(trans * (opacity * falloff_ref[:, at]))
        colour_high, colour_low = split(vals[8:16, at])
        image = image + (
            mm_nt(colour_high, weight_high)
            + mm_nt(colour_low, weight_high)
            + mm_nt(colour_high, weight_low)
        )
    image_ref[0] = image
    grad_image = 2.0 * (image - target_ref[0])
    grand_total = jnp.sum(grad_image * image, axis=0, keepdims=True)
    grand_total = jnp.transpose(jnp.broadcast_to(grand_total, (128, pixels)))
    grand_total = jnp.concatenate([grand_total] * (SB // 128), axis=1)
    grad_high, grad_low = split(grad_image)
    turned_high, turned_low = split(jnp.transpose(grad_image))

    spent = jnp.zeros((pixels, 1), F32)
    for blk in range(blocks):
        at = slice(blk * SB, (blk + 1) * SB)
        mean_x, mean_y = vals[0:1, at], vals[1:2, at]
        conic_a, conic_b, conic_c = vals[2:3, at], vals[3:4, at], vals[4:5, at]
        opacity = vals[5:6, at]
        dx = centres - mean_x
        dy = centres - mean_y
        colour_high, colour_low = split(vals[8:16, at])
        shading = (
            mm(turned_high, colour_high) + mm(turned_high, colour_low) + mm(turned_low, colour_high)
        )
        shade_ref[...] = shading
        weight = trans_ref[:, at] * (opacity * falloff_ref[:, at])
        weight_high, weight_low = split(weight)
        grads[8:16, at] = (
            mm(grad_high, weight_high) + mm(grad_low, weight_high) + mm(grad_high, weight_low)
        )
        high, low = split(weight * shading)
        before = mm(high, inclusive) + mm(low, inclusive) + spent
        spent = before[:, SB - 1 : SB]
        before_ref[...] = grand_total - before
        power0 = jnp.zeros((SIDE, SB), F32)
        power1 = power0
        power2 = power0
        opaque = power0
        for y in range(side_rows):
            rows = slice(y * SIDE, (y + 1) * SIDE)
            falloff = falloff_ref[rows, at]
            alpha = opacity * falloff
            grad_alpha = trans_ref[rows, at] * shade_ref[rows, :] - before_ref[rows, :] / (
                1.0 - alpha
            )
            opaque = opaque + grad_alpha * falloff
            power = grad_alpha * alpha
            power0 = power0 - power
            moment = power * dy[y : y + 1]
            power1 = power1 - moment
            power2 = power2 - moment * dy[y : y + 1]
        across = power0 * dx
        sum_x = jnp.sum(across, axis=0, keepdims=True)
        sum_y = jnp.sum(power1, axis=0, keepdims=True)
        grads[0:1, at] = -(conic_a * sum_x + conic_b * sum_y)
        grads[1:2, at] = -(conic_c * sum_y + conic_b * sum_x)
        grads[2:3, at] = 0.5 * jnp.sum(across * dx, axis=0, keepdims=True)
        grads[3:4, at] = jnp.sum(power1 * dx, axis=0, keepdims=True)
        grads[4:5, at] = 0.5 * jnp.sum(power2, axis=0, keepdims=True)
        grads[5:6, at] = jnp.sum(opaque, axis=0, keepdims=True) * live[:, at]

    for ch in range(CH):
        part = slice(ch * devices, (ch + 1) * devices)
        row = ch if ch < 6 else ch + 2
        high, low = split(jnp.where(mine, grads[row : row + 1, :], 0.0))
        sent = mm_nt(high, places) + mm_nt(low, places)

        @pl.when(tile == 0)
        def _():
            out_ref[part, :] = sent

        @pl.when(tile > 0)
        def _():
            out_ref[part, :] += sent


def scatter_kernel(ask_ref, grad_ref, out_ref, row_ref, column_ref):
    rows, width = out_ref.shape[1], out_ref.shape[2]
    count = ask_ref.shape[1]
    step = min(1024, count)

    @pl.when(pl.program_id(0) == 0)
    def _():
        def build(j, none):
            at = pl.ds(pl.multiple_of(j * step, step), step)
            index = ask_ref[:, at]
            row_ref[:, at] = one_hot(index >> 8, rows)
            column_ref[:, at] = one_hot(index & (width - 1), width)
            return none

        lax.fori_loop(0, count // step, build, 0)

    total = jnp.zeros((rows, width), F32)

    def add(j, total):
        at = pl.ds(pl.multiple_of(j * step, step), step)
        grad = jnp.broadcast_to(grad_ref[0, :, at], (16, step))
        high, low = split(grad)
        tops = row_ref[:, at]
        column = column_ref[:, at]
        left_high = jnp.concatenate([tops[k : k + 16] * high for k in range(0, rows, 16)], axis=0)
        left_low = jnp.concatenate([tops[k : k + 16] * low for k in range(0, rows, 16)], axis=0)
        return total + (mm_nt(left_high, column) + mm_nt(left_low, column))

    out_ref[0] = lax.fori_loop(0, count // step, add, total)


def body(splat_params, list_owner, list_slot, list_length, target):
    devices = lax.axis_size(("row", "col"))
    tiles, slots = list_slot.shape
    entries = tiles * slots
    splats = splat_params.shape[1]
    pixels = target.shape[2]
    cap = 2 * entries // devices
    total = devices * cap
    width = 256
    rows = splats // width
    owners = list_owner.reshape(1, entries)
    requests, ranks = pl.pallas_call(
        plan_kernel,
        out_shape=(
            jax.ShapeDtypeStruct((devices, cap), jnp.int32),
            jax.ShapeDtypeStruct((1, entries), jnp.int32),
        ),
        name="plan",
    )(owners, list_slot.reshape(1, entries))
    asked = lax.all_to_all(requests, ("row", "col"), split_axis=0, concat_axis=0, tiled=True)
    steps = total // LANES
    table = splat_params.reshape(CH * rows, width)
    looked = pl.pallas_call(
        gather_kernel,
        grid=(steps,),
        in_specs=[
            pl.BlockSpec((1, 1, LANES), lambda i: (i, 0, 0)),
            pl.BlockSpec((CH * rows, width), lambda i: (0, 0)),
        ],
        out_specs=pl.BlockSpec((1, CH, LANES), lambda i: (i, 0, 0)),
        out_shape=jax.ShapeDtypeStruct((steps, CH, LANES), F32),
        scratch_shapes=[
            pltpu.VMEM((CH * rows, width), BF16),
            pltpu.VMEM((CH * rows, width), BF16),
        ],
        name="lookup",
    )(asked.reshape(steps, 1, LANES), table)
    per = LANES // cap
    looked = looked.reshape(steps, CH, per, cap).transpose(0, 2, 1, 3).reshape(devices, CH, cap)
    answer = lax.all_to_all(looked, ("row", "col"), split_axis=0, concat_axis=0, tiled=True)
    replies = answer.transpose(1, 0, 2).reshape(CH * devices, cap)
    targets = jnp.pad(target.transpose(1, 0, 2), ((0, 0), (0, 4), (0, 0)))
    images, outgoing = pl.pallas_call(
        render_kernel,
        grid=(tiles,),
        in_specs=[
            pl.BlockSpec(memory_space=pltpu.SMEM),
            pl.BlockSpec((1, 1, slots), lambda i: (i, 0, 0)),
            pl.BlockSpec((1, 1, slots), lambda i: (i, 0, 0)),
            pl.BlockSpec((CH * devices, cap), lambda i: (0, 0)),
            pl.BlockSpec((1, 8, pixels), lambda i: (i, 0, 0)),
        ],
        out_specs=(
            pl.BlockSpec((1, 8, pixels), lambda i: (i, 0, 0)),
            pl.BlockSpec((CH * devices, cap), lambda i: (0, 0)),
        ),
        out_shape=(
            jax.ShapeDtypeStruct((tiles, 8, pixels), F32),
            jax.ShapeDtypeStruct((CH * devices, cap), F32),
        ),
        scratch_shapes=[
            pltpu.VMEM((16, slots), F32),
            pltpu.VMEM((16, slots), F32),
            pltpu.VMEM((pixels, slots), F32),
            pltpu.VMEM((pixels, slots), F32),
            pltpu.VMEM((pixels, SB), BF16),
            pltpu.VMEM((pixels, SB), BF16),
            pltpu.VMEM((pixels, SB), F32),
            pltpu.VMEM((pixels, SB), F32),
        ],
        name="render",
    )(
        list_length,
        owners.reshape(tiles, 1, slots),
        ranks.reshape(tiles, 1, slots),
        replies,
        targets,
    )
    rendered = images[:, :4].transpose(1, 0, 2)
    sending = outgoing.reshape(CH, devices, cap).transpose(1, 0, 2)
    incoming = lax.all_to_all(sending, ("row", "col"), split_axis=0, concat_axis=0, tiled=True)
    arrived = incoming.transpose(1, 0, 2).reshape(CH, 1, total)
    splat_grads = pl.pallas_call(
        scatter_kernel,
        grid=(CH,),
        in_specs=[
            pl.BlockSpec((1, total), lambda i: (0, 0)),
            pl.BlockSpec((1, 1, total), lambda i: (i, 0, 0)),
        ],
        out_specs=pl.BlockSpec((1, rows, width), lambda i: (i, 0, 0)),
        out_shape=jax.ShapeDtypeStruct((CH, rows, width), F32),
        scratch_shapes=[
            pltpu.VMEM((rows, total), BF16),
            pltpu.VMEM((width, total), BF16),
        ],
        name="accumulate",
    )(asked.reshape(1, total), arrived)
    return (rendered, splat_grads.reshape(CH, splats))


def solution(mesh):
    in_specs = (
        P(None, ("row", "col")),
        P(("row", "col"), None, None),
        P(("row", "col"), None),
        P(("row", "col")),
        P(None, ("row", "col"), None),
    )
    out_specs = (P(None, ("row", "col"), None), P(None, ("row", "col")))
    return jax.shard_map(body, mesh=mesh, in_specs=in_specs, out_specs=out_specs, check_vma=False)
```

```python
import functools

import jax
import jax.numpy as jnp
from jax import lax
from jax.experimental import pallas as pl
from jax.experimental.pallas import tpu as pltpu
from jax.sharding import PartitionSpec as P

SIDE = 16
SB = 256
LANES = 256
CH = 10
F32 = jnp.float32
BF16 = jnp.bfloat16
NT = (((1,), (1,)), ((), ()))


def iota(shape, dim):
    return lax.broadcasted_iota(jnp.int32, shape, dim)


def split(x):
    high = x.astype(BF16)
    return high, (x - high.astype(F32)).astype(BF16)


def mm(a, b):
    return jnp.dot(a, b, preferred_element_type=F32)


def mm_nt(a, b):
    return lax.dot_general(a, b, NT, preferred_element_type=F32)


def one_hot(index, size):
    return jnp.where(iota((size, index.shape[1]), 0) == index, 1.0, 0.0).astype(BF16)


def plan_kernel(own_ref, slot_ref, req_ref, rank_ref):
    devices, cap = req_ref.shape
    entries = own_ref.shape[1]
    strict = jnp.where(iota((SB, SB), 0) < iota((SB, SB), 1), 1.0, 0.0).astype(BF16)
    carry = jnp.zeros((devices, 1), F32)
    high = jnp.zeros((devices, cap), F32)
    low = jnp.zeros((devices, cap), F32)
    for j in range(entries // SB):
        part = slice(j * SB, (j + 1) * SB)
        mine = iota((devices, SB), 0) == own_ref[:, part]
        ones = jnp.where(mine, 1.0, 0.0)
        count = mm(ones.astype(BF16), strict) + carry
        rank = jnp.sum(ones * count, axis=0, keepdims=True).astype(jnp.int32)
        carry = carry + jnp.sum(ones, axis=1, keepdims=True)
        rank_ref[:, part] = rank
        slots = slot_ref[:, part]
        places = one_hot(rank, cap)
        slot_high = (slots >> 8).astype(F32)
        slot_low = (slots & 255).astype(F32)
        high = high + mm_nt(jnp.where(mine, slot_high, 0.0).astype(BF16), places)
        low = low + mm_nt(jnp.where(mine, slot_low, 0.0).astype(BF16), places)
    req_ref[...] = (high * 256.0 + low).astype(jnp.int32)


def gather_kernel(ask_ref, table_ref, out_ref, parts_ref):
    width = table_ref.shape[1]
    rows = table_ref.shape[0] // CH

    @pl.when(pl.program_id(0) == 0)
    def _():
        for ch in range(CH):
            part = slice(ch * rows, (ch + 1) * rows)
            high, low = split(table_ref[part, :])
            parts_ref[part, :width] = high
            parts_ref[part, width:] = low

    index = ask_ref[0]
    column = one_hot(index & (width - 1), width)
    row = iota((rows, index.shape[1]), 0) == (index >> 8)
    found = mm(parts_ref[...], jnp.concatenate([column, column], axis=0))
    for ch in range(CH):
        picked = jnp.where(row, found[ch * rows : (ch + 1) * rows], 0.0)
        out_ref[0, ch : ch + 1, :] = jnp.sum(picked, axis=0, keepdims=True)


def render_kernel(
    length_ref, own_ref, rank_ref, reply_ref, target_ref, image_ref, out_ref,
    vals, grads, falloff_ref, trans_ref, high_ref, low_ref, shade_ref, before_ref, pack_ref,
):
    tile = pl.program_id(0)
    devices = reply_ref.shape[0] // CH
    cap = reply_ref.shape[1]
    slots = own_ref.shape[2]
    pixels = target_ref.shape[2]
    blocks = slots // SB
    length = length_ref[tile]
    mine = iota((devices, slots), 0) == own_ref[0]
    places = one_hot(rank_ref[0], cap)
    reply_high, reply_low = split(reply_ref[...])
    fetched = mm(reply_high, places) + mm(reply_low, places)
    vals[...] = jnp.zeros_like(vals)
    live = jnp.where(iota((1, slots), 1) < length, 1.0, 0.0)
    for ch in range(CH):
        part = slice(ch * devices, (ch + 1) * devices)
        value = jnp.sum(jnp.where(mine, fetched[part], 0.0), axis=0, keepdims=True)
        if ch == 5:
            value = value * live
        row = ch if ch < 6 else ch + 2
        vals[row : row + 1, :] = value

    strict = jnp.where(iota((SB, SB), 0) < iota((SB, SB), 1), 1.0, 0.0).astype(BF16)
    inclusive = jnp.where(iota((SB, SB), 0) <= iota((SB, SB), 1), 1.0, 0.0).astype(BF16)
    centres = iota((SIDE, SB), 0).astype(F32) + 0.5
    side_rows = pixels // SIDE

    carry = jnp.zeros((pixels, 1), F32)
    image = jnp.zeros((pixels, 8), F32)
    for blk in range(blocks):
        at = slice(blk * SB, (blk + 1) * SB)
        dx = centres - vals[0:1, at]
        dy = centres - vals[1:2, at]
        ex = 0.5 * vals[2:3, at] * dx * dx
        ey = 0.5 * vals[4:5, at] * dy * dy
        bdy = vals[3:4, at] * dy
        opacity = vals[5:6, at]
        for y in range(side_rows):
            rows = slice(y * SIDE, (y + 1) * SIDE)
            exponent = ex + ey[y : y + 1] + dx * bdy[y : y + 1]
            falloff = jnp.exp(-exponent)
            falloff_ref[rows, at] = falloff
            keep = jnp.log(1.0 - opacity * falloff)
            high, low = split(keep)
            high_ref[rows, :] = high
            low_ref[rows, :] = low
        total = mm(high_ref[...], strict) + mm(low_ref[...], strict) + carry
        last = high_ref[:, SB - 128 :].astype(F32) + low_ref[:, SB - 128 :].astype(F32)
        carry = total[:, SB - 1 : SB] + last[:, 127:128]
        trans = jnp.exp(total)
        trans_ref[:, at] = trans
        weight_high, weight_low = split(trans * (opacity * falloff_ref[:, at]))
        colour_high, colour_low = split(vals[8:16, at])
        image = image + (
            mm_nt(weight_high, colour_high)
            + mm_nt(weight_high, colour_low)
            + mm_nt(weight_low, colour_high)
        )
    rendered = jnp.transpose(image)
    image_ref[0] = rendered
    grad_image = 2.0 * (rendered - target_ref[0])
    grad_high, grad_low = split(grad_image)
    grad_wide = grad_high.astype(F32)
    grad_rest = grad_image - grad_wide
    turned = jnp.transpose(jnp.concatenate([grad_wide, grad_wide, grad_rest, grad_image], axis=0))
    turned_parts = turned.astype(BF16)
    grand_total = jnp.sum(jnp.transpose(grad_image) * image, axis=1, keepdims=True)

    spent = jnp.zeros((pixels, 1), F32)
    for blk in range(blocks):
        at = slice(blk * SB, (blk + 1) * SB)
        mean_x, mean_y = vals[0:1, at], vals[1:2, at]
        conic_a, conic_b, conic_c = vals[2:3, at], vals[3:4, at], vals[4:5, at]
        opacity = vals[5:6, at]
        dx = centres - mean_x
        dy = centres - mean_y
        colours = vals[8:16, at]
        colour_wide = colours.astype(BF16).astype(F32)
        colour_parts = jnp.concatenate(
            [colour_wide, colours - colour_wide, colour_wide, jnp.zeros_like(colours)], axis=0
        ).astype(BF16)
        shading = mm(turned_parts, colour_parts)
        shade_ref[...] = shading
        weight = trans_ref[:, at] * (opacity * falloff_ref[:, at])
        weight_high, weight_low = split(weight)
        grads[8:16, at] = (
            mm(grad_high, weight_high) + mm(grad_low, weight_high) + mm(grad_high, weight_low)
        )
        high, low = split(weight * shading)
        before = mm(high, inclusive) + mm(low, inclusive) + spent
        spent = before[:, SB - 1 : SB]
        before_ref[...] = grand_total - before
        power0 = jnp.zeros((SIDE, SB), F32)
        power1 = power0
        power2 = power0
        opaque = power0
        for y in range(side_rows):
            rows = slice(y * SIDE, (y + 1) * SIDE)
            falloff = falloff_ref[rows, at]
            alpha = opacity * falloff
            grad_alpha = trans_ref[rows, at] * shade_ref[rows, :] - before_ref[rows, :] / (
                1.0 - alpha
            )
            opaque = opaque + grad_alpha * falloff
            power = grad_alpha * alpha
            power0 = power0 - power
            moment = power * dy[y : y + 1]
            power1 = power1 - moment
            power2 = power2 - moment * dy[y : y + 1]
        across = power0 * dx
        sum_x = jnp.sum(across, axis=0, keepdims=True)
        sum_y = jnp.sum(power1, axis=0, keepdims=True)
        grads[0:1, at] = -(conic_a * sum_x + conic_b * sum_y)
        grads[1:2, at] = -(conic_c * sum_y + conic_b * sum_x)
        grads[2:3, at] = 0.5 * jnp.sum(across * dx, axis=0, keepdims=True)
        grads[3:4, at] = jnp.sum(power1 * dx, axis=0, keepdims=True)
        grads[4:5, at] = 0.5 * jnp.sum(power2, axis=0, keepdims=True)
        grads[5:6, at] = jnp.sum(opaque, axis=0, keepdims=True) * live[:, at]

    for ch in range(CH):
        part = slice(ch * devices, (ch + 1) * devices)
        row = ch if ch < 6 else ch + 2
        high, low = split(jnp.where(mine, grads[row : row + 1, :], 0.0))
        pack_ref[0, part, :] = high
        pack_ref[1, part, :] = low
    sent = mm_nt(pack_ref[0], places) + mm_nt(pack_ref[1], places)

    @pl.when(tile == 0)
    def _():
        out_ref[...] = sent

    @pl.when(tile > 0)
    def _():
        out_ref[...] += sent


def scatter_kernel(ask_ref, grad_ref, out_ref, high_ref, low_ref, sum_ref):
    step = pl.program_id(0)
    halves = sum_ref.shape[0]
    width = halves * 128
    rows = sum_ref.shape[1] // CH
    index = ask_ref[...]
    column = one_hot(index & (width - 1), width)
    tops = one_hot(index >> 8, rows)
    for ch in range(CH):
        grad = jnp.broadcast_to(grad_ref[ch : ch + 1, :], (16, index.shape[1]))
        high, low = split(grad)
        for k in range(0, rows, 16):
            part = slice(ch * rows + k, ch * rows + k + 16)
            high_ref[part, :] = tops[k : k + 16] * high
            low_ref[part, :] = tops[k : k + 16] * low
    total = mm_nt(high_ref[...], column) + mm_nt(low_ref[...], column)

    @pl.when(step == 0)
    def _():
        for k in range(halves):
            sum_ref[k] = total[:, k * 128 : (k + 1) * 128]

    @pl.when(step > 0)
    def _():
        for k in range(halves):
            sum_ref[k] += total[:, k * 128 : (k + 1) * 128]

    @pl.when(step == pl.num_programs(0) - 1)
    def _():
        for q in range(rows):
            for k in range(halves):
                at = slice((q * halves + k) * 128, (q * halves + k + 1) * 128)
                out_ref[0:8, at] = sum_ref[k, pl.ds(q, 8, stride=rows), :]
                out_ref[8:CH, at] = sum_ref[k, pl.ds(8 * rows + q, CH - 8, stride=rows), :]


def body(splat_params, list_owner, list_slot, list_length, target):
    devices = lax.axis_size(("row", "col"))
    tiles, slots = list_slot.shape
    entries = tiles * slots
    splats = splat_params.shape[1]
    pixels = target.shape[2]
    cap = 2 * entries // devices
    total = devices * cap
    width = 256
    rows = splats // width
    owners = list_owner.reshape(1, entries)
    requests, ranks = pl.pallas_call(
        plan_kernel,
        out_shape=(
            jax.ShapeDtypeStruct((devices, cap), jnp.int32),
            jax.ShapeDtypeStruct((1, entries), jnp.int32),
        ),
        name="plan",
    )(owners, list_slot.reshape(1, entries))
    asked = lax.all_to_all(requests, ("row", "col"), split_axis=0, concat_axis=0, tiled=True)
    steps = total // LANES
    table = splat_params.reshape(CH * rows, width)
    looked = pl.pallas_call(
        gather_kernel,
        grid=(steps,),
        in_specs=[
            pl.BlockSpec((1, 1, LANES), lambda i: (i, 0, 0)),
            pl.BlockSpec((CH * rows, width), lambda i: (0, 0)),
        ],
        out_specs=pl.BlockSpec((1, CH, LANES), lambda i: (i, 0, 0)),
        out_shape=jax.ShapeDtypeStruct((steps, CH, LANES), F32),
        scratch_shapes=[
            pltpu.VMEM((CH * rows, 2 * width), BF16),
        ],
        name="lookup",
    )(asked.reshape(steps, 1, LANES), table)
    per = LANES // cap
    looked = looked.reshape(steps, CH, per, cap).transpose(0, 2, 1, 3).reshape(devices, CH, cap)
    answer = lax.all_to_all(looked, ("row", "col"), split_axis=0, concat_axis=0, tiled=True)
    replies = answer.transpose(1, 0, 2).reshape(CH * devices, cap)
    targets = jnp.pad(target.transpose(1, 0, 2), ((0, 0), (0, 4), (0, 0)))
    images, outgoing = pl.pallas_call(
        render_kernel,
        grid=(tiles,),
        in_specs=[
            pl.BlockSpec(memory_space=pltpu.SMEM),
            pl.BlockSpec((1, 1, slots), lambda i: (i, 0, 0)),
            pl.BlockSpec((1, 1, slots), lambda i: (i, 0, 0)),
            pl.BlockSpec((CH * devices, cap), lambda i: (0, 0)),
            pl.BlockSpec((1, 8, pixels), lambda i: (i, 0, 0)),
        ],
        out_specs=(
            pl.BlockSpec((1, 8, pixels), lambda i: (i, 0, 0)),
            pl.BlockSpec((CH * devices, cap), lambda i: (0, 0)),
        ),
        out_shape=(
            jax.ShapeDtypeStruct((tiles, 8, pixels), F32),
            jax.ShapeDtypeStruct((CH * devices, cap), F32),
        ),
        scratch_shapes=[
            pltpu.VMEM((16, slots), F32),
            pltpu.VMEM((16, slots), F32),
            pltpu.VMEM((pixels, slots), F32),
            pltpu.VMEM((pixels, slots), F32),
            pltpu.VMEM((pixels, SB), BF16),
            pltpu.VMEM((pixels, SB), BF16),
            pltpu.VMEM((pixels, SB), F32),
            pltpu.VMEM((pixels, SB), F32),
            pltpu.VMEM((2, CH * devices, slots), BF16),
        ],
        name="render",
    )(
        list_length,
        owners.reshape(tiles, 1, slots),
        ranks.reshape(tiles, 1, slots),
        replies,
        targets,
    )
    rendered = images[:, :4].transpose(1, 0, 2)
    sending = outgoing.reshape(CH, devices, cap).transpose(1, 0, 2)
    incoming = lax.all_to_all(sending, ("row", "col"), split_axis=0, concat_axis=0, tiled=True)
    arrived = incoming.transpose(1, 0, 2).reshape(CH, total)
    chunk = min(512, total)
    splat_grads = pl.pallas_call(
        scatter_kernel,
        grid=(total // chunk,),
        in_specs=[
            pl.BlockSpec((1, chunk), lambda i: (0, i)),
            pl.BlockSpec((CH, chunk), lambda i: (0, i)),
        ],
        out_specs=pl.BlockSpec((CH, splats), lambda i: (0, 0)),
        out_shape=jax.ShapeDtypeStruct((CH, splats), F32),
        scratch_shapes=[
            pltpu.VMEM((CH * rows, chunk), BF16),
            pltpu.VMEM((CH * rows, chunk), BF16),
            pltpu.VMEM((width // 128, CH * rows, 128), F32),
        ],
        name="accumulate",
    )(asked.reshape(1, total), arrived)
    return (rendered, splat_grads)


def solution(mesh):
    in_specs = (
        P(None, ("row", "col")),
        P(("row", "col"), None, None),
        P(("row", "col"), None),
        P(("row", "col")),
        P(None, ("row", "col"), None),
    )
    out_specs = (P(None, ("row", "col"), None), P(None, ("row", "col")))
    return jax.shard_map(body, mesh=mesh, in_specs=in_specs, out_specs=out_specs, check_vma=False)
```

```python
import functools

import jax
import jax.numpy as jnp
from jax import lax
from jax.experimental import pallas as pl
from jax.experimental.pallas import tpu as pltpu
from jax.sharding import PartitionSpec as P

SIDE = 16
SB = 256
LANES = 256
CH = 10
EARLY = 6
TOP = 8
F32 = jnp.float32
BF16 = jnp.bfloat16
NT = (((1,), (1,)), ((), ()))


def iota(shape, dim):
    return lax.broadcasted_iota(jnp.int32, shape, dim)


def split(x):
    high = x.astype(BF16)
    return high, (x - high.astype(F32)).astype(BF16)


def mm(a, b):
    return jnp.dot(a, b, preferred_element_type=F32)


def mm_nt(a, b):
    return lax.dot_general(a, b, NT, preferred_element_type=F32)


def one_hot(index, size):
    return jnp.where(iota((size, index.shape[1]), 0) == index, 1.0, 0.0).astype(BF16)


def plan_kernel(own_ref, slot_ref, req_ref, rank_ref):
    devices, cap = req_ref.shape
    entries = own_ref.shape[1]
    strict = jnp.where(iota((SB, SB), 0) < iota((SB, SB), 1), 1.0, 0.0).astype(BF16)
    carry = jnp.zeros((devices, 1), F32)
    high = jnp.zeros((devices, cap), F32)
    low = jnp.zeros((devices, cap), F32)
    for j in range(entries // SB):
        part = slice(j * SB, (j + 1) * SB)
        mine = iota((devices, SB), 0) == own_ref[:, part]
        ones = jnp.where(mine, 1.0, 0.0)
        count = mm(ones.astype(BF16), strict) + carry
        rank = jnp.sum(ones * count, axis=0, keepdims=True).astype(jnp.int32)
        carry = carry + jnp.sum(ones, axis=1, keepdims=True)
        rank_ref[:, part] = rank
        slots = slot_ref[:, part]
        places = one_hot(rank, cap)
        slot_high = (slots >> 8).astype(F32)
        slot_low = (slots & 255).astype(F32)
        high = high + mm_nt(jnp.where(mine, slot_high, 0.0).astype(BF16), places)
        low = low + mm_nt(jnp.where(mine, slot_low, 0.0).astype(BF16), places)
    req_ref[...] = (high * 256.0 + low).astype(jnp.int32)


def gather_kernel(ask_ref, table_ref, out_ref, parts_ref):
    width = table_ref.shape[1]
    channels = out_ref.shape[1]
    rows = table_ref.shape[0] // channels

    @pl.when(pl.program_id(0) == 0)
    def _():
        for ch in range(channels):
            part = slice(ch * rows, (ch + 1) * rows)
            high, low = split(table_ref[part, :])
            parts_ref[part, :width] = high
            parts_ref[part, width:] = low

    index = ask_ref[0]
    column = one_hot(index & (width - 1), width)
    row = iota((rows, index.shape[1]), 0) == (index >> 8)
    found = mm(parts_ref[...], jnp.concatenate([column, column], axis=0))
    for ch in range(channels):
        picked = jnp.where(row, found[ch * rows : (ch + 1) * rows], 0.0)
        out_ref[0, ch : ch + 1, :] = jnp.sum(picked, axis=0, keepdims=True)


def render_kernel(
    length_ref, own_ref, rank_ref, reply_ref, target_ref, image_ref, out_ref,
    vals, grads, falloff_ref, trans_ref, high_ref, low_ref, shade_ref, before_ref, pack_ref,
):
    tile = pl.program_id(0)
    devices = reply_ref.shape[0] // CH
    cap = reply_ref.shape[1]
    slots = own_ref.shape[2]
    pixels = target_ref.shape[2]
    blocks = slots // SB
    length = length_ref[tile]
    mine = iota((devices, slots), 0) == own_ref[0]
    places = one_hot(rank_ref[0], cap)
    reply_high, reply_low = split(reply_ref[...])
    fetched = mm(reply_high, places) + mm(reply_low, places)
    vals[...] = jnp.zeros_like(vals)
    live = jnp.where(iota((1, slots), 1) < length, 1.0, 0.0)
    for ch in range(CH):
        part = slice(ch * devices, (ch + 1) * devices)
        value = jnp.sum(jnp.where(mine, fetched[part], 0.0), axis=0, keepdims=True)
        if ch == 5:
            value = value * live
        row = ch if ch < 6 else ch + 2
        vals[row : row + 1, :] = value

    strict = jnp.where(iota((SB, SB), 0) < iota((SB, SB), 1), 1.0, 0.0).astype(BF16)
    inclusive = jnp.where(iota((SB, SB), 0) <= iota((SB, SB), 1), 1.0, 0.0).astype(BF16)
    centres = iota((SIDE, SB), 0).astype(F32) + 0.5
    side_rows = pixels // SIDE

    carry = jnp.zeros((pixels, 1), F32)
    image = jnp.zeros((pixels, 8), F32)
    for blk in range(blocks):
        at = slice(blk * SB, (blk + 1) * SB)
        dx = centres - vals[0:1, at]
        dy = centres - vals[1:2, at]
        ex = 0.5 * vals[2:3, at] * dx * dx
        ey = 0.5 * vals[4:5, at] * dy * dy
        bdy = vals[3:4, at] * dy
        opacity = vals[5:6, at]
        for y in range(side_rows):
            rows = slice(y * SIDE, (y + 1) * SIDE)
            exponent = ex + ey[y : y + 1] + dx * bdy[y : y + 1]
            falloff = jnp.exp(-exponent)
            falloff_ref[rows, at] = falloff
            keep = jnp.log(1.0 - opacity * falloff)
            high, low = split(keep)
            high_ref[rows, :] = high
            low_ref[rows, :] = low
        total = mm(high_ref[...], strict) + mm(low_ref[...], strict) + carry
        last = high_ref[:, SB - 128 :].astype(F32) + low_ref[:, SB - 128 :].astype(F32)
        carry = total[:, SB - 1 : SB] + last[:, 127:128]
        trans = jnp.exp(total)
        trans_ref[:, at] = trans
        weight_high, weight_low = split(trans * (opacity * falloff_ref[:, at]))
        colour_high, colour_low = split(vals[8:16, at])
        image = image + (
            mm_nt(weight_high, colour_high)
            + mm_nt(weight_high, colour_low)
            + mm_nt(weight_low, colour_high)
        )
    rendered = jnp.transpose(image)
    image_ref[0] = rendered
    grad_image = 2.0 * (rendered - target_ref[0])
    grad_high, grad_low = split(grad_image)
    grad_wide = grad_high.astype(F32)
    grad_rest = grad_image - grad_wide
    turned = jnp.transpose(jnp.concatenate([grad_wide, grad_wide, grad_rest, grad_image], axis=0))
    turned_parts = turned.astype(BF16)
    grand_total = jnp.sum(jnp.transpose(grad_image) * image, axis=1, keepdims=True)

    spent = jnp.zeros((pixels, 1), F32)
    for blk in range(blocks):
        at = slice(blk * SB, (blk + 1) * SB)
        mean_x, mean_y = vals[0:1, at], vals[1:2, at]
        conic_a, conic_b, conic_c = vals[2:3, at], vals[3:4, at], vals[4:5, at]
        opacity = vals[5:6, at]
        dx = centres - mean_x
        dy = centres - mean_y
        colours = vals[8:16, at]
        colour_wide = colours.astype(BF16).astype(F32)
        colour_parts = jnp.concatenate(
            [colour_wide, colours - colour_wide, colour_wide, jnp.zeros_like(colours)], axis=0
        ).astype(BF16)
        shading = mm(turned_parts, colour_parts)
        shade_ref[...] = shading
        weight = trans_ref[:, at] * (opacity * falloff_ref[:, at])
        weight_high, weight_low = split(weight)
        grads[8:16, at] = (
            mm(grad_high, weight_high) + mm(grad_low, weight_high) + mm(grad_high, weight_low)
        )
        high, low = split(weight * shading)
        before = mm(high, inclusive) + mm(low, inclusive) + spent
        spent = before[:, SB - 1 : SB]
        before_ref[...] = grand_total - before
        power0 = jnp.zeros((SIDE, SB), F32)
        power1 = power0
        power2 = power0
        opaque = power0
        for y in range(side_rows):
            rows = slice(y * SIDE, (y + 1) * SIDE)
            falloff = falloff_ref[rows, at]
            alpha = opacity * falloff
            grad_alpha = trans_ref[rows, at] * shade_ref[rows, :] - before_ref[rows, :] / (
                1.0 - alpha
            )
            opaque = opaque + grad_alpha * falloff
            power = grad_alpha * alpha
            power0 = power0 - power
            moment = power * dy[y : y + 1]
            power1 = power1 - moment
            power2 = power2 - moment * dy[y : y + 1]
        across = power0 * dx
        sum_x = jnp.sum(across, axis=0, keepdims=True)
        sum_y = jnp.sum(power1, axis=0, keepdims=True)
        grads[0:1, at] = -(conic_a * sum_x + conic_b * sum_y)
        grads[1:2, at] = -(conic_c * sum_y + conic_b * sum_x)
        grads[2:3, at] = 0.5 * jnp.sum(across * dx, axis=0, keepdims=True)
        grads[3:4, at] = jnp.sum(power1 * dx, axis=0, keepdims=True)
        grads[4:5, at] = 0.5 * jnp.sum(power2, axis=0, keepdims=True)
        grads[5:6, at] = jnp.sum(opaque, axis=0, keepdims=True) * live[:, at]

    for ch in range(CH):
        part = slice(ch * devices, (ch + 1) * devices)
        row = ch if ch < 6 else ch + 2
        high, low = split(jnp.where(mine, grads[row : row + 1, :], 0.0))
        pack_ref[0, part, :] = high
        pack_ref[1, part, :] = low
    sent = mm_nt(pack_ref[0], places) + mm_nt(pack_ref[1], places)

    @pl.when(tile == 0)
    def _():
        out_ref[...] = sent

    @pl.when(tile > 0)
    def _():
        out_ref[...] += sent


def scatter_kernel(ask_ref, grad_ref, *refs):
    out_ref, high_ref, low_ref, sum_ref = refs[-4:]
    channels = grad_ref.shape[0]
    step = pl.program_id(0)
    halves = sum_ref.shape[0]
    width = halves * 128
    rows = sum_ref.shape[1] // channels
    index = ask_ref[...]
    column = one_hot(index & (width - 1), width)
    tops = one_hot(index >> 8, rows)
    for ch in range(channels):
        grad = jnp.broadcast_to(grad_ref[ch : ch + 1, :], (16, index.shape[1]))
        high, low = split(grad)
        for k in range(0, rows, 16):
            part = slice(ch * rows + k, ch * rows + k + 16)
            high_ref[part, :] = tops[k : k + 16] * high
            low_ref[part, :] = tops[k : k + 16] * low
    total = mm_nt(high_ref[...], column) + mm_nt(low_ref[...], column)

    @pl.when(step == 0)
    def _():
        for k in range(halves):
            sum_ref[k] = total[:, k * 128 : (k + 1) * 128]

    @pl.when(step > 0)
    def _():
        for k in range(halves):
            sum_ref[k] += total[:, k * 128 : (k + 1) * 128]

    @pl.when(step == pl.num_programs(0) - 1)
    def _():
        for q in range(rows):
            for k in range(halves):
                at = slice((q * halves + k) * 128, (q * halves + k + 1) * 128)
                out_ref[0:channels, at] = sum_ref[k, pl.ds(q, channels, stride=rows), :]


def body(splat_params, list_owner, list_slot, list_length, target):
    devices = lax.axis_size(("row", "col"))
    tiles, slots = list_slot.shape
    entries = tiles * slots
    splats = splat_params.shape[1]
    pixels = target.shape[2]
    cap = 2 * entries // devices
    total = devices * cap
    width = 256
    rows = splats // width
    owners = list_owner.reshape(1, entries)
    requests, ranks = pl.pallas_call(
        plan_kernel,
        out_shape=(
            jax.ShapeDtypeStruct((devices, cap), jnp.int32),
            jax.ShapeDtypeStruct((1, entries), jnp.int32),
        ),
        name="plan",
    )(owners, list_slot.reshape(1, entries))
    asked = lax.all_to_all(requests, ("row", "col"), split_axis=0, concat_axis=0, tiled=True)
    steps = total // LANES
    per = LANES // cap

    def lookup(params, asked):
        channels = params.shape[0]
        table = params.reshape(channels * rows, width)
        looked = pl.pallas_call(
            gather_kernel,
            grid=(steps,),
            in_specs=[
                pl.BlockSpec((1, 1, LANES), lambda i: (i, 0, 0)),
                pl.BlockSpec((channels * rows, width), lambda i: (0, 0)),
            ],
            out_specs=pl.BlockSpec((1, channels, LANES), lambda i: (i, 0, 0)),
            out_shape=jax.ShapeDtypeStruct((steps, channels, LANES), F32),
            scratch_shapes=[pltpu.VMEM((channels * rows, 2 * width), BF16)],
            cost_estimate=pl.CostEstimate(
                flops=4 * channels * splats * total,
                bytes_accessed=4 * channels * (splats + total),
                transcendentals=0,
            ),
            name="lookup",
        )(asked.reshape(steps, 1, LANES), table)
        looked = looked.reshape(steps, channels, per, cap).transpose(0, 2, 1, 3)
        return looked.reshape(devices, channels, cap)

    def exchange(values):
        return lax.all_to_all(values, ("row", "col"), split_axis=0, concat_axis=0, tiled=True)

    first = lookup(splat_params[:EARLY], asked)
    first, asked = lax.optimization_barrier((first, asked))
    first_answer = exchange(first)
    second_answer = exchange(lookup(splat_params[EARLY:], asked))
    answer = jnp.concatenate([first_answer, second_answer], axis=1)
    replies = answer.transpose(1, 0, 2).reshape(CH * devices, cap)
    targets = jnp.pad(target.transpose(1, 0, 2), ((0, 0), (0, 4), (0, 0)))
    images, outgoing = pl.pallas_call(
        render_kernel,
        grid=(tiles,),
        in_specs=[
            pl.BlockSpec(memory_space=pltpu.SMEM),
            pl.BlockSpec((1, 1, slots), lambda i: (i, 0, 0)),
            pl.BlockSpec((1, 1, slots), lambda i: (i, 0, 0)),
            pl.BlockSpec((CH * devices, cap), lambda i: (0, 0)),
            pl.BlockSpec((1, 8, pixels), lambda i: (i, 0, 0)),
        ],
        out_specs=(
            pl.BlockSpec((1, 8, pixels), lambda i: (i, 0, 0)),
            pl.BlockSpec((CH * devices, cap), lambda i: (0, 0)),
        ),
        out_shape=(
            jax.ShapeDtypeStruct((tiles, 8, pixels), F32),
            jax.ShapeDtypeStruct((CH * devices, cap), F32),
        ),
        scratch_shapes=[
            pltpu.VMEM((16, slots), F32),
            pltpu.VMEM((16, slots), F32),
            pltpu.VMEM((pixels, slots), F32),
            pltpu.VMEM((pixels, slots), F32),
            pltpu.VMEM((pixels, SB), BF16),
            pltpu.VMEM((pixels, SB), BF16),
            pltpu.VMEM((pixels, SB), F32),
            pltpu.VMEM((pixels, SB), F32),
            pltpu.VMEM((2, CH * devices, slots), BF16),
        ],
        name="render",
    )(
        list_length,
        owners.reshape(tiles, 1, slots),
        ranks.reshape(tiles, 1, slots),
        replies,
        targets,
    )
    rendered = images[:, :4].transpose(1, 0, 2)
    outgoing = outgoing.reshape(CH, devices, cap)
    chunk = min(512, total)

    def accumulate(incoming, block, held):
        channels = incoming.shape[1]
        arrived = incoming.transpose(1, 0, 2).reshape(channels, total)
        return pl.pallas_call(
            scatter_kernel,
            grid=(total // chunk,),
            in_specs=[
                pl.BlockSpec((1, chunk), lambda i: (0, i)),
                pl.BlockSpec((channels, chunk), lambda i: (0, i)),
            ]
            + [pl.BlockSpec(memory_space=pl.ANY)] * len(held),
            out_specs=pl.BlockSpec((TOP, splats), lambda i: (block, 0)),
            out_shape=jax.ShapeDtypeStruct((CH, splats), F32),
            scratch_shapes=[
                pltpu.VMEM((channels * rows, chunk), BF16),
                pltpu.VMEM((channels * rows, chunk), BF16),
                pltpu.VMEM((width // 128, channels * rows, 128), F32),
            ],
            input_output_aliases={2: 0} if held else {},
            cost_estimate=pl.CostEstimate(
                flops=4 * channels * splats * total,
                bytes_accessed=4 * channels * (splats + total),
                transcendentals=0,
            ),
            name="accumulate",
        )(asked.reshape(1, total), arrived, *held)

    rest = exchange(outgoing[TOP:].transpose(1, 0, 2))
    main = exchange(outgoing[:TOP].transpose(1, 0, 2))
    held = accumulate(rest, 1, ())
    splat_grads = accumulate(main, 0, (held,))
    return (rendered, splat_grads)


def solution(mesh):
    in_specs = (
        P(None, ("row", "col")),
        P(("row", "col"), None, None),
        P(("row", "col"), None),
        P(("row", "col")),
        P(None, ("row", "col"), None),
    )
    out_specs = (P(None, ("row", "col"), None), P(None, ("row", "col")))
    return jax.shard_map(body, mesh=mesh, in_specs=in_specs, out_specs=out_specs, check_vma=False)
```
